32 devices in a mesh: row: 16 (over z, y, core), col: 2 (over x).
Axes of the slice: x: 2, y: 2, z: 4, core: 2. Of those that a mesh axis runs over, the one named last changes fastest.
Arguments:
- acts: bfloat16 [1024, 4096], P(None, 'col'), may hold values from -6 to 6
- grads: bfloat16 [1024, 8192], P(None, 'row'), may hold values from -0.1875 to 0.1875
- row_roots: bfloat16 [8192, 1024], P('row'), as said below
- col_stats: float32 [1024, 4096], P('row', 'col'), as said below
Outputs:
- update: bfloat16 [8192, 4096], P('row', 'col')
- new_stats: float32 [1024, 4096], P('row', 'col')
- new_roots: float32 [1024, 4096], P('row', 'col')
The draws below stay inside these ranges and needn't reach their ends.
Inputs may be any that keep to these rules, and one draw needn't show every extreme that they name: `col_stats`: each block of 1024 columns is symmetric positive definite. `row_roots`: each block of 1024 rows is symmetric.
All inputs are finite; a program needn't handle non-finite values.
Results may differ from the reference program's by a relative error of at most 0.0015.
The reference program's roundings to bfloat16 on the way (of `grad`, `whitened` and `roots_half`) count: a program that leaves them out, or rounds other values in their place, can miss the bound.
Values may be sent and summed in bfloat16 or wider, within the bound.
A program may use at most 128 MiB of HBM per device.

```python
import jax
import jax.numpy as jnp
from jax import lax

BLK = 1024
TOK = 1024
DOUT = 8192
DIN = 4096


def symmetric_blocks(key, count, size, lower, upper):
    key_diag, key_noise = jax.random.split(key)
    diagonal = jnp.exp(jax.random.uniform(key_diag, (count, size), jnp.float32, jnp.log(lower), jnp.log(upper)))
    noise = jax.random.normal(key_noise, (count, size, size), jnp.float32) * (0.3 / jnp.sqrt(1.0 * size))
    sym = 0.5 * (noise + jnp.swapaxes(noise, 1, 2))
    inner = jnp.eye(size, dtype=jnp.float32)[None] + sym
    roots_diag = jnp.sqrt(diagonal)
    return roots_diag[:, :, None] * inner * roots_diag[:, None, :]


def draw_row_roots(key, part):
    blocks = symmetric_blocks(jax.random.fold_in(key, 11), DOUT // BLK, BLK, 0.5, 2.0)
    return blocks.reshape(DOUT, BLK).astype(jnp.bfloat16)


def draw_col_stats(key, part):
    blocks = symmetric_blocks(jax.random.fold_in(key, 23), DIN // BLK, BLK, 1.0, 3.0)
    return blocks.transpose(1, 0, 2).reshape(BLK, DIN)


def block_scale(rng, extent, pieces, least, high):
    level = 1.0
    for axis_at, blocks in pieces:
        steps = jax.random.uniform(jax.random.fold_in(jax.random.fold_in(rng, 6), axis_at), (blocks,), jnp.float32, least / len(pieces), high / len(pieces))
        level = level * jnp.repeat(jnp.exp(steps), extent[axis_at] // blocks).reshape((-1,) + (1,) * (len(extent) - 1 - axis_at))
    return level


def scatter_about(key, dims, spread, limit, shards=(), kind=jnp.bfloat16):
    array = spread * jax.random.normal(key, dims, jnp.float32)
    if shards:
        array = array * block_scale(key, dims, shards, -0.22, 0.18)
    return jnp.clip(array, -limit, limit).astype(kind)


def setup_inputs(seed: int = 0) -> dict:
    streams_of = jax.random.split(jax.random.key(seed), 5)
    acts = scatter_about(streams_of[0], (TOK, DIN), 1.0, 6.0, ((1, 2),))
    grads = scatter_about(streams_of[1], (TOK, DOUT), TOK ** -0.5, 0.1875, ((1, 16),))
    row_roots = draw_row_roots(jax.random.fold_in(streams_of[4], 71), 0)
    col_stats = draw_col_stats(jax.random.fold_in(streams_of[4], 71), 0)
    return dict(acts=acts, grads=grads, row_roots=row_roots, col_stats=col_stats)


decay_rate = 0.75
damping = 0.001
epsilon = 1e-06

def inverse_root(stat):
    size = stat.shape[0]
    identity = jnp.eye(size, dtype=stat.dtype)
    shifted = stat + damping * identity
    norm_scale = 2.0 * jnp.trace(shifted) / size
    start_iterate = shifted / norm_scale
    first_factor = 1.5 * identity - 0.5 * start_iterate
    second_iterate = jnp.dot(start_iterate, first_factor, precision=lax.Precision.HIGHEST)
    product_full = jnp.dot(first_factor, second_iterate, precision=lax.Precision.HIGHEST)
    second_factor = 1.5 * identity - 0.5 * product_full
    root_full = jnp.dot(second_factor, first_factor, precision=lax.Precision.HIGHEST)
    return root_full / jnp.sqrt(norm_scale)

def reference(acts, grads, row_roots, col_stats):
    contract_first = (((0,), (0,)), ((), ()))
    grad = lax.dot_general(grads, acts, contract_first, preferred_element_type=jnp.float32).astype(jnp.bfloat16)
    row_blocks = DOUT // BLK
    col_blocks = DIN // BLK
    roots_three = row_roots.reshape(row_blocks, BLK, BLK)
    grad_three = grad.reshape(row_blocks, BLK, DIN)

    def whiten(pair):
        return jnp.dot(pair[0], pair[1], preferred_element_type=jnp.float32).astype(jnp.bfloat16)
    whitened = lax.map(whiten, (roots_three, grad_three)).reshape(DOUT, DIN)
    columns = whitened.reshape(DOUT, col_blocks, BLK).transpose(1, 0, 2)
    old_three = col_stats.reshape(BLK, col_blocks, BLK).transpose(1, 0, 2)
    mix = (1.0 - decay_rate) / DOUT

    def column_block(pair):
        wcols, old = pair
        part = lax.dot_general(wcols, wcols, contract_first, preferred_element_type=jnp.float32)
        stat = decay_rate * old + mix * part
        return (stat, inverse_root(stat))
    stats_three, roots_new = lax.map(column_block, (columns, old_three))
    roots_half = roots_new.astype(jnp.bfloat16)

    def precondition(pair):
        return jnp.dot(pair[0], pair[1], preferred_element_type=jnp.float32)
    product = lax.map(precondition, (columns, roots_half))
    product = product.transpose(1, 0, 2).reshape(DOUT, DIN)
    grad_square = jnp.sum(jnp.square(grad.astype(jnp.float32)))
    prod_square = jnp.sum(jnp.square(product))
    update = (product * jnp.sqrt(grad_square / (prod_square + epsilon))).astype(jnp.bfloat16)
    new_stats = stats_three.transpose(1, 0, 2).reshape(BLK, DIN)
    new_roots = roots_new.transpose(1, 0, 2).reshape(BLK, DIN)
    return (update, new_stats, new_roots)
```

```python
import functools

import jax
import jax.numpy as jnp
from jax import lax
from jax.experimental import pallas as pl
from jax.experimental.pallas import tpu as pltpu
from jax.sharding import PartitionSpec as P


decay_rate = 0.75
damping = 0.001
epsilon = 1e-06


def partner(block, axis, bit):
    count = lax.axis_size(axis)
    route = []
    for low in range(count):
        high = low | 1 << bit
        if high != low and high < count:
            route += [(low, high), (high, low)]
    return lax.ppermute(block, axis, route)


def exchange_kernel(axes, sizes, x_ref, out_ref, held, send_sems, recv_sems):
    count = 1
    me = 0
    for axis, size in zip(axes, sizes):
        me = me * size + lax.axis_index(axis)
        count *= size

    def place(peer):
        spot = {}
        for axis, size in reversed(list(zip(axes, sizes))):
            spot[axis] = lax.rem(peer, size)
            peer = lax.div(peer, size)
        return spot

    peers = [place(lax.rem(me + step, count)) for step in range(1, count)]
    barrier = pltpu.get_barrier_semaphore()
    for peer in peers:
        pl.semaphore_signal(barrier, inc=1, device_id=peer, device_id_type=pl.DeviceIdType.MESH)
    pl.semaphore_wait(barrier, count - 1)
    copies = []
    for index, peer in enumerate(peers):
        copy = pltpu.make_async_remote_copy(
            src_ref=x_ref,
            dst_ref=held.at[me],
            send_sem=send_sems.at[index],
            recv_sem=recv_sems.at[index],
            device_id=peer,
            device_id_type=pl.DeviceIdType.MESH,
        )
        copy.start()
        copies.append(copy)
    held[me] = x_ref[...]
    for copy in copies:
        copy.wait()
    total = held[0]
    for index in range(1, count):
        total = total + held[index]
    out_ref[...] = total


def small_sum(packet, axes, collective_id):
    sizes = tuple(lax.axis_size(axis) for axis in axes)
    count = 1
    for size in sizes:
        count *= size
    return pl.pallas_call(
        functools.partial(exchange_kernel, axes, sizes),
        out_shape=jax.ShapeDtypeStruct(packet.shape, packet.dtype),
        in_specs=[pl.BlockSpec(memory_space=pltpu.VMEM)],
        out_specs=pl.BlockSpec(memory_space=pltpu.VMEM),
        scratch_shapes=[
            pltpu.VMEM((count,) + packet.shape, packet.dtype),
            pltpu.SemaphoreType.DMA((count - 1,)),
            pltpu.SemaphoreType.DMA((count - 1,)),
        ],
        compiler_params=pltpu.CompilerParams(collective_id=collective_id, has_side_effects=True),
    )(packet)


def bit_orders(index_block, bits):
    far = list(range(2, bits))
    if index_block % 2 == 0:
        return [0, 1] + far
    return [0] + far + [1]


def halve(parts, mine, bit, position):
    low = lax.index_in_dim(parts, 0, position, keepdims=False)
    high = lax.index_in_dim(parts, 1, position, keepdims=False)
    upper = mine == 1
    keep = jnp.where(upper, high, low)
    send = jnp.where(upper, low, high).astype(jnp.bfloat16)
    return keep.astype(jnp.float32) + partner(send, "row", bit).astype(jnp.float32)


def reduce_rows(part, index_block, me, bits, stat_rows):
    width = part.shape[1]
    left = list(range(bits - 1, -1, -1))
    current = part.reshape((2,) * bits + (stat_rows, width))
    for bit in bit_orders(index_block, bits):
        position = left.index(bit)
        left.remove(bit)
        current = halve(current, (me >> bit) & 1, bit, position)
    return current


def gather_rows(piece, index_block, me, bits):
    stat_rows, width = piece.shape
    current = piece[None]
    order = []
    for bit in reversed(bit_orders(index_block, bits)):
        current = jnp.concatenate([current, partner(current, "row", bit)], 0)
        order.append(bit)
    rows = []
    for target in range(1 << bits):
        apart = me ^ target
        slot = 0
        for at, bit in enumerate(order):
            slot = slot + (((apart >> bit) & 1) << at)
        rows.append(lax.dynamic_index_in_dim(current, slot, 0, keepdims=False))
    return jnp.concatenate(rows, 0)


def shards(acts, grads, row_roots, col_stats):
    contract_first = (((0,), (0,)), ((), ()))
    block_size = row_roots.shape[1]
    weight_rows = grads.shape[1]
    weight_cols = acts.shape[1]
    stat_rows = col_stats.shape[0]
    block_count = weight_cols // block_size
    row_count = lax.axis_size("row")
    bits = row_count.bit_length() - 1
    total_rows = weight_rows * row_count
    me = lax.axis_index("row")
    other_grads = partner(grads, "row", 0)
    own_tile = lax.dot_general(
        grads, acts, contract_first, preferred_element_type=jnp.float32
    ).astype(jnp.bfloat16)
    other_tile = lax.dot_general(
        other_grads, acts, contract_first, preferred_element_type=jnp.float32
    ).astype(jnp.bfloat16)
    is_lower = me % 2 == 0
    paired = jnp.where(
        is_lower,
        jnp.concatenate([own_tile, other_tile], 0),
        jnp.concatenate([other_tile, own_tile], 0),
    )
    whitened = jnp.dot(row_roots, paired, preferred_element_type=jnp.float32).astype(jnp.bfloat16)
    mix = (1.0 - decay_rate) / total_rows
    first_row = me * stat_rows
    row_iota = lax.broadcasted_iota(jnp.int32, (stat_rows, block_size), 0) + first_row
    col_iota = lax.broadcasted_iota(jnp.int32, (stat_rows, block_size), 1)
    on_diagonal = row_iota == col_iota
    identity_rows = on_diagonal.astype(jnp.float32)

    def block(array, index):
        return array[:, index * block_size : (index + 1) * block_size]

    blocks = range(block_count)
    old_diagonal = jnp.concatenate(
        [jnp.sum(jnp.where(on_diagonal, block(col_stats, k), 0.0), 0) for k in blocks]
    )
    squares = jnp.sum(jnp.square(whitened.astype(jnp.float32)), 0)
    packet = (decay_rate * old_diagonal + mix * squares).reshape(-1, 128)
    diagonal = small_sum(packet, ("row",), 0).reshape(block_count, block_size)

    stats = []
    for k in blocks:
        columns = block(whitened, k)
        part = lax.dot_general(columns, columns, contract_first, preferred_element_type=jnp.float32)
        summed = reduce_rows(part.astype(jnp.bfloat16), k, me, bits, stat_rows)
        mixed = decay_rate * block(col_stats, k) + mix * summed
        stats.append(jnp.where(on_diagonal, diagonal[k][None], mixed))
    new_stats = jnp.concatenate(stats, 1)

    root_pieces = []
    for k in blocks:
        off_rows = jnp.where(on_diagonal, 0.0, stats[k]).astype(jnp.bfloat16)
        off = gather_rows(off_rows, k, me, bits)
        shifted = diagonal[k] + damping
        scale = 2.0 * jnp.sum(shifted) / block_size

        def times_start(rows):
            high = rows.astype(jnp.bfloat16)
            low = (rows - high.astype(jnp.float32)).astype(jnp.bfloat16)
            both = jnp.dot(
                jnp.concatenate([high, low], 0), off, preferred_element_type=jnp.float32
            )
            return (both[:stat_rows] + both[stat_rows:] + rows * shifted[None]) / scale

        start_rows = jnp.where(on_diagonal, shifted[None], stats[k]) / scale
        first = 1.5 * identity_rows - 0.5 * start_rows
        step = times_start(first)
        product_rows = 1.5 * step - 0.5 * times_start(step)
        second = 1.5 * identity_rows - 0.5 * product_rows
        root_rows = 1.5 * second - 0.5 * times_start(second)
        root_pieces.append(root_rows / jnp.sqrt(scale))
    new_roots = jnp.concatenate(root_pieces, 1)
    terms = []
    for k in blocks:
        right = gather_rows(root_pieces[k].astype(jnp.bfloat16), k, me, bits)
        terms.append(jnp.dot(block(whitened, k), right, preferred_element_type=jnp.float32))
    product = jnp.concatenate(terms, 1)
    grad_square = jnp.sum(jnp.square(own_tile.astype(jnp.float32)))
    prod_square = sum(jnp.sum(jnp.square(term)) for term in terms)
    lane = lax.broadcasted_iota(jnp.int32, (8, 128), 1)
    norms = jnp.where(lane == 0, grad_square, jnp.where(lane == 1, prod_square, 0.0))
    totals = small_sum(norms, ("row", "col"), 1)
    update = (product * jnp.sqrt(totals[0, 0] / (totals[0, 1] + epsilon))).astype(jnp.bfloat16)
    return (update, new_stats, new_roots)


def solution(mesh):
    return jax.shard_map(
        shards,
        mesh=mesh,
        in_specs=(P(None, "col"), P(None, "row"), P("row", None), P("row", "col")),
        out_specs=(P("row", "col"), P("row", "col"), P("row", "col")),
        check_vma=False,
    )
```

```python
import functools

import jax
import jax.numpy as jnp
from jax import lax
from jax.experimental import pallas as pl
from jax.experimental.pallas import tpu as pltpu
from jax.sharding import PartitionSpec as P


decay_rate = 0.75
damping = 0.001
epsilon = 1e-06


def partner(block, axis, bit):
    count = lax.axis_size(axis)
    route = []
    for low in range(count):
        high = low | 1 << bit
        if high != low and high < count:
            route += [(low, high), (high, low)]
    return lax.ppermute(block, axis, route)


def exchange_kernel(axes, sizes, x_ref, out_ref, held, send_sems, recv_sems):
    count = 1
    me = 0
    for axis, size in zip(axes, sizes):
        me = me * size + lax.axis_index(axis)
        count *= size

    def place(peer):
        spot = {}
        for axis, size in reversed(list(zip(axes, sizes))):
            spot[axis] = lax.rem(peer, size)
            peer = lax.div(peer, size)
        return spot

    peers = [place(lax.rem(me + step, count)) for step in range(1, count)]
    barrier = pltpu.get_barrier_semaphore()
    for peer in peers:
        pl.semaphore_signal(barrier, inc=1, device_id=peer, device_id_type=pl.DeviceIdType.MESH)
    pl.semaphore_wait(barrier, count - 1)
    copies = []
    for index, peer in enumerate(peers):
        copy = pltpu.make_async_remote_copy(
            src_ref=x_ref,
            dst_ref=held.at[me],
            send_sem=send_sems.at[index],
            recv_sem=recv_sems.at[index],
            device_id=peer,
            device_id_type=pl.DeviceIdType.MESH,
        )
        copy.start()
        copies.append(copy)
    held[me] = x_ref[...]
    for copy in copies:
        copy.wait()
    total = held[0]
    for index in range(1, count):
        total = total + held[index]
    out_ref[...] = total


def small_sum(packet, axes, collective_id):
    sizes = tuple(lax.axis_size(axis) for axis in axes)
    count = 1
    for size in sizes:
        count *= size
    return pl.pallas_call(
        functools.partial(exchange_kernel, axes, sizes),
        out_shape=jax.ShapeDtypeStruct(packet.shape, packet.dtype),
        in_specs=[pl.BlockSpec(memory_space=pltpu.VMEM)],
        out_specs=pl.BlockSpec(memory_space=pltpu.VMEM),
        scratch_shapes=[
            pltpu.VMEM((count,) + packet.shape, packet.dtype),
            pltpu.SemaphoreType.DMA((count - 1,)),
            pltpu.SemaphoreType.DMA((count - 1,)),
        ],
        compiler_params=pltpu.CompilerParams(collective_id=collective_id, has_side_effects=True),
    )(packet)


def bit_orders(index_block, bits):
    far = list(range(2, bits))
    if index_block % 2 == 0:
        return [0, 1] + far
    return [0] + far + [1]


def halve(parts, mine, bit, position):
    low = lax.index_in_dim(parts, 0, position, keepdims=False)
    high = lax.index_in_dim(parts, 1, position, keepdims=False)
    upper = mine == 1
    keep = jnp.where(upper, high, low)
    send = jnp.where(upper, low, high).astype(jnp.bfloat16)
    return keep.astype(jnp.float32) + partner(send, "row", bit).astype(jnp.float32)


def reduce_rows(part, index_block, me, bits, stat_rows):
    width = part.shape[1]
    left = list(range(bits - 1, -1, -1))
    current = part.reshape((2,) * bits + (stat_rows, width))
    for bit in bit_orders(index_block, bits):
        position = left.index(bit)
        left.remove(bit)
        current = halve(current, (me >> bit) & 1, bit, position)
    return current


def gather_kernel(count, summed, x_ref, *refs):
    if summed:
        packet_ref, out_ref, sum_ref, held, own_sem, sends, recvs, small_sends, small_recvs = refs
    else:
        out_ref, own_sem, sends, recvs = refs
    depth = count // 4
    me = lax.axis_index("row")
    mesh_ids = pl.DeviceIdType.MESH
    near = lax.rem(me, 4)
    tall = lax.div(me, 4)
    y_peer = me + 2 - 4 * lax.rem(lax.div(me, 2), 2)
    core_peer = me + 1 - 2 * lax.rem(me, 2)
    origins = [lax.rem(tall - step + depth, depth) * 4 + near for step in range(depth)]
    y_origins = [lax.rem(tall - step + depth, depth) * 4 + lax.rem(near + 2, 4) for step in range(depth)]
    z_peers = [lax.rem(tall + step, depth) * 4 + near for step in range(1, depth)]
    everyone = [lax.rem(me + step, count) for step in range(1, count)]
    greeted = everyone if summed else z_peers + [y_peer, core_peer]
    barrier = pltpu.get_barrier_semaphore()
    for peer in greeted:
        pl.semaphore_signal(barrier, inc=1, device_id={"row": peer}, device_id_type=mesh_ids)
    pl.semaphore_wait(barrier, len(greeted))

    def push(source, slot, peer, index):
        copy = pltpu.make_async_remote_copy(
            src_ref=source,
            dst_ref=out_ref.at[slot],
            send_sem=sends.at[index],
            recv_sem=recvs.at[index],
            device_id={"row": peer},
            device_id_type=mesh_ids,
        )
        copy.start()
        return copy

    small = []
    if summed:
        for index, peer in enumerate(everyone):
            copy = pltpu.make_async_remote_copy(
                src_ref=packet_ref,
                dst_ref=held.at[me],
                send_sem=small_sends.at[index],
                recv_sem=small_recvs.at[index],
                device_id={"row": peer},
                device_id_type=mesh_ids,
            )
            copy.start()
            small.append(copy)
        held[me] = packet_ref[...]
    along_z = [push(x_ref, me, peer, at) for at, peer in enumerate(z_peers)]
    base = depth - 1
    along_y = [push(x_ref, me, y_peer, base)]
    across = [push(x_ref, me, core_peer, base + depth)]
    own = pltpu.make_async_copy(x_ref, out_ref.at[me], own_sem)
    own.start()
    late = []

    def forward_y(step):
        along_y[step].wait_recv()
        slot = y_origins[step]
        late.append(push(out_ref.at[slot], slot, core_peer, base + 2 * depth + step))

    for step in range(1, depth):
        along_z[step - 1].wait_recv()
        slot = origins[step]
        along_y.append(push(out_ref.at[slot], slot, y_peer, base + step))
        across.append(push(out_ref.at[slot], slot, core_peer, base + depth + step))
        forward_y(step - 1)
    forward_y(depth - 1)
    if summed:
        for copy in small:
            copy.wait()
        total = held[0]
        for index in range(1, count):
            total = total + held[index]
        sum_ref[...] = total
    for copy in across + late:
        copy.wait_recv()
    for copy in along_z + along_y + across + late:
        copy.wait_send()
    own.wait()


def gather_rows(piece, collective_id, packet=None):
    count = lax.axis_size("row")
    stat_rows, width = piece.shape
    copies = 4 * (count // 4) - 1
    summed = packet is not None
    vmem = pl.BlockSpec(memory_space=pltpu.VMEM)
    gathered = jax.ShapeDtypeStruct((count,) + piece.shape, piece.dtype)
    scratch = [
        pltpu.SemaphoreType.DMA,
        pltpu.SemaphoreType.DMA((copies,)),
        pltpu.SemaphoreType.DMA((copies,)),
    ]
    out_shape, out_specs = [gathered], [pl.BlockSpec(memory_space=pl.ANY)]
    if summed:
        out_shape.append(jax.ShapeDtypeStruct(packet.shape, packet.dtype))
        out_specs.append(vmem)
        scratch = [pltpu.VMEM((count,) + packet.shape, packet.dtype)] + scratch
        scratch += [pltpu.SemaphoreType.DMA((count - 1,)), pltpu.SemaphoreType.DMA((count - 1,))]
    operands = [piece] + ([packet] if summed else [])
    results = pl.pallas_call(
        functools.partial(gather_kernel, count, summed),
        out_shape=out_shape,
        in_specs=[vmem] * len(operands),
        out_specs=out_specs,
        scratch_shapes=scratch,
        compiler_params=pltpu.CompilerParams(collective_id=collective_id, has_side_effects=True),
    )(*operands)
    return [results[0].reshape(count * stat_rows, width)] + list(results[1:])


def shards(acts, grads, row_roots, col_stats):
    contract_first = (((0,), (0,)), ((), ()))
    block_size = row_roots.shape[1]
    weight_rows = grads.shape[1]
    weight_cols = acts.shape[1]
    stat_rows = col_stats.shape[0]
    block_count = weight_cols // block_size
    row_count = lax.axis_size("row")
    bits = row_count.bit_length() - 1
    total_rows = weight_rows * row_count
    me = lax.axis_index("row")
    other_grads = partner(grads, "row", 0)
    own_tile = lax.dot_general(
        grads, acts, contract_first, preferred_element_type=jnp.float32
    ).astype(jnp.bfloat16)
    other_tile = lax.dot_general(
        other_grads, acts, contract_first, preferred_element_type=jnp.float32
    ).astype(jnp.bfloat16)
    is_lower = me % 2 == 0
    paired = jnp.where(
        is_lower,
        jnp.concatenate([own_tile, other_tile], 0),
        jnp.concatenate([other_tile, own_tile], 0),
    )
    whitened = jnp.dot(row_roots, paired, preferred_element_type=jnp.float32).astype(jnp.bfloat16)
    mix = (1.0 - decay_rate) / total_rows
    first_row = me * stat_rows
    row_iota = lax.broadcasted_iota(jnp.int32, (stat_rows, block_size), 0) + first_row
    col_iota = lax.broadcasted_iota(jnp.int32, (stat_rows, block_size), 1)
    on_diagonal = row_iota == col_iota
    identity_rows = on_diagonal.astype(jnp.float32)

    def block(array, index):
        return array[:, index * block_size : (index + 1) * block_size]

    blocks = range(block_count)
    old_diagonal = jnp.concatenate(
        [jnp.sum(jnp.where(on_diagonal, block(col_stats, k), 0.0), 0) for k in blocks]
    )
    squares = jnp.sum(jnp.square(whitened.astype(jnp.float32)), 0)
    packet = (decay_rate * old_diagonal + mix * squares).reshape(-1, 128)

    stats = []
    for k in blocks:
        columns = block(whitened, k)
        part = lax.dot_general(columns, columns, contract_first, preferred_element_type=jnp.float32)
        summed = reduce_rows(part.astype(jnp.bfloat16), k, me, bits, stat_rows)
        mixed = decay_rate * block(col_stats, k) + mix * summed
        stats.append(jnp.where(on_diagonal, 0.0, mixed))
    off_full, diagonal = gather_rows(jnp.concatenate(stats, 1).astype(jnp.bfloat16), 0, packet)
    diagonal = diagonal.reshape(block_count, block_size)
    stats = [jnp.where(on_diagonal, diagonal[k][None], stats[k]) for k in blocks]
    new_stats = jnp.concatenate(stats, 1)

    root_pieces = []
    for k in blocks:
        off = block(off_full, k)
        shifted = diagonal[k] + damping
        scale = 2.0 * jnp.sum(shifted) / block_size

        def times_start(rows):
            high = rows.astype(jnp.bfloat16)
            low = (rows - high.astype(jnp.float32)).astype(jnp.bfloat16)
            both = jnp.dot(
                jnp.concatenate([high, low], 0), off, preferred_element_type=jnp.float32
            )
            return (both[:stat_rows] + both[stat_rows:] + rows * shifted[None]) / scale

        start_rows = jnp.where(on_diagonal, shifted[None], stats[k]) / scale
        first = 1.5 * identity_rows - 0.5 * start_rows
        step = times_start(first)
        product_rows = 1.5 * step - 0.5 * times_start(step)
        second = 1.5 * identity_rows - 0.5 * product_rows
        root_rows = 1.5 * second - 0.5 * times_start(second)
        root_pieces.append(root_rows / jnp.sqrt(scale))
    new_roots = jnp.concatenate(root_pieces, 1)
    (roots_full,) = gather_rows(new_roots.astype(jnp.bfloat16), 2)
    terms = []
    for k in blocks:
        right = block(roots_full, k)
        terms.append(jnp.dot(block(whitened, k), right, preferred_element_type=jnp.float32))
    product = jnp.concatenate(terms, 1)
    grad_square = jnp.sum(jnp.square(own_tile.astype(jnp.float32)))
    prod_square = sum(jnp.sum(jnp.square(term)) for term in terms)
    lane = lax.broadcasted_iota(jnp.int32, (8, 128), 1)
    norms = jnp.where(lane == 0, grad_square, jnp.where(lane == 1, prod_square, 0.0))
    totals = small_sum(norms, ("row", "col"), 1)
    update = (product * jnp.sqrt(totals[0, 0] / (totals[0, 1] + epsilon))).astype(jnp.bfloat16)
    return (update, new_stats, new_roots)


def solution(mesh):
    return jax.shard_map(
        shards,
        mesh=mesh,
        in_specs=(P(None, "col"), P(None, "row"), P("row", None), P("row", "col")),
        out_specs=(P("row", "col"), P("row", "col"), P("row", "col")),
        check_vma=False,
    )
```

```python
import functools

import jax
import jax.numpy as jnp
from jax import lax
from jax.experimental import pallas as pl
from jax.experimental.pallas import tpu as pltpu
from jax.sharding import PartitionSpec as P


decay_rate = 0.75
damping = 0.001
epsilon = 1e-06


def partner(block, axis, bit):
    count = lax.axis_size(axis)
    route = []
    for low in range(count):
        high = low | 1 << bit
        if high != low and high < count:
            route += [(low, high), (high, low)]
    return lax.ppermute(block, axis, route)


def exchange_kernel(axes, sizes, x_ref, out_ref, held, send_sems, recv_sems):
    count = 1
    me = 0
    for axis, size in zip(axes, sizes):
        me = me * size + lax.axis_index(axis)
        count *= size

    def place(peer):
        spot = {}
        for axis, size in reversed(list(zip(axes, sizes))):
            spot[axis] = lax.rem(peer, size)
            peer = lax.div(peer, size)
        return spot

    peers = [place(lax.rem(me + step, count)) for step in range(1, count)]
    barrier = pltpu.get_barrier_semaphore()
    for peer in peers:
        pl.semaphore_signal(barrier, inc=1, device_id=peer, device_id_type=pl.DeviceIdType.MESH)
    pl.semaphore_wait(barrier, count - 1)
    copies = []
    for index, peer in enumerate(peers):
        copy = pltpu.make_async_remote_copy(
            src_ref=x_ref,
            dst_ref=held.at[me],
            send_sem=send_sems.at[index],
            recv_sem=recv_sems.at[index],
            device_id=peer,
            device_id_type=pl.DeviceIdType.MESH,
        )
        copy.start()
        copies.append(copy)
    held[me] = x_ref[...]
    for copy in copies:
        copy.wait()
    total = held[0]
    for index in range(1, count):
        total = total + held[index]
    out_ref[...] = total


def small_sum(packet, axes, collective_id):
    sizes = tuple(lax.axis_size(axis) for axis in axes)
    count = 1
    for size in sizes:
        count *= size
    return pl.pallas_call(
        functools.partial(exchange_kernel, axes, sizes),
        out_shape=jax.ShapeDtypeStruct(packet.shape, packet.dtype),
        in_specs=[pl.BlockSpec(memory_space=pltpu.VMEM)],
        out_specs=pl.BlockSpec(memory_space=pltpu.VMEM),
        scratch_shapes=[
            pltpu.VMEM((count,) + packet.shape, packet.dtype),
            pltpu.SemaphoreType.DMA((count - 1,)),
            pltpu.SemaphoreType.DMA((count - 1,)),
        ],
        compiler_params=pltpu.CompilerParams(collective_id=collective_id, has_side_effects=True),
    )(packet)


def bit_orders(index_block, bits):
    far = list(range(2, bits))
    if index_block % 2 == 0:
        return [0, 1] + far
    return [0] + far + [1]


def halve(parts, mine, bit, position):
    low = lax.index_in_dim(parts, 0, position, keepdims=False)
    high = lax.index_in_dim(parts, 1, position, keepdims=False)
    upper = mine == 1
    keep = jnp.where(upper, high, low)
    send = jnp.where(upper, low, high).astype(jnp.bfloat16)
    return keep.astype(jnp.float32) + partner(send, "row", bit).astype(jnp.float32)


def reduce_rows(part, index_block, me, bits, stat_rows):
    width = part.shape[1]
    left = list(range(bits - 1, -1, -1))
    current = part.reshape((2,) * bits + (stat_rows, width))
    for bit in bit_orders(index_block, bits):
        position = left.index(bit)
        left.remove(bit)
        current = halve(current, (me >> bit) & 1, bit, position)
    return current


def gather_kernel(count, summed, x_ref, *refs):
    if summed:
        packet_ref, out_ref, sum_ref, held, own_sem, sends, recvs, small_sends, small_recvs = refs
    else:
        out_ref, own_sem, sends, recvs = refs
    depth = count // 4
    me = lax.axis_index("row")
    mesh_ids = pl.DeviceIdType.MESH
    near = lax.rem(me, 4)
    tall = lax.div(me, 4)
    y_peer = me + 2 - 4 * lax.rem(lax.div(me, 2), 2)
    core_peer = me + 1 - 2 * lax.rem(me, 2)
    origins = [lax.bitwise_xor(tall, step) * 4 + near for step in range(depth)]
    y_origins = [lax.bitwise_xor(tall, step) * 4 + lax.rem(near + 2, 4) for step in range(depth)]
    hops = [1 << bit for bit in range(depth.bit_length() - 1)]
    z_peers = [origins[hop] for hop in hops]
    everyone = [lax.rem(me + step, count) for step in range(1, count)]
    greeted = everyone if summed else z_peers + [y_peer, core_peer]
    barrier = pltpu.get_barrier_semaphore()
    for peer in greeted:
        pl.semaphore_signal(barrier, inc=1, device_id={"row": peer}, device_id_type=mesh_ids)
    pl.semaphore_wait(barrier, len(greeted))

    def push(source, slot, peer, index):
        copy = pltpu.make_async_remote_copy(
            src_ref=source,
            dst_ref=out_ref.at[slot],
            send_sem=sends.at[index],
            recv_sem=recvs.at[index],
            device_id={"row": peer},
            device_id_type=mesh_ids,
        )
        copy.start()
        return copy

    small = []
    if summed:
        for index, peer in enumerate(everyone):
            copy = pltpu.make_async_remote_copy(
                src_ref=packet_ref,
                dst_ref=held.at[me],
                send_sem=small_sends.at[index],
                recv_sem=small_recvs.at[index],
                device_id={"row": peer},
                device_id_type=mesh_ids,
            )
            copy.start()
            small.append(copy)
        held[me] = packet_ref[...]
    along_z = {hop: push(x_ref, me, origins[hop], hop - 1) for hop in hops}
    base = depth - 1
    along_y = [push(x_ref, me, y_peer, base)]
    across = [push(x_ref, me, core_peer, base + depth)]
    own = pltpu.make_async_copy(x_ref, out_ref.at[me], own_sem)
    own.start()
    late = []

    def forward_y(step):
        along_y[step].wait_recv()
        slot = y_origins[step]
        late.append(push(out_ref.at[slot], slot, core_peer, base + 2 * depth + step))

    for step in range(1, depth):
        along_z[step].wait_recv()
        slot = origins[step]
        for hop in hops:
            if hop < (step & -step):
                along_z[step + hop] = push(out_ref.at[slot], slot, origins[hop], step + hop - 1)
        along_y.append(push(out_ref.at[slot], slot, y_peer, base + step))
        across.append(push(out_ref.at[slot], slot, core_peer, base + depth + step))
        forward_y(step - 1)
    forward_y(depth - 1)
    if summed:
        for copy in small:
            copy.wait()
        total = held[0]
        for index in range(1, count):
            total = total + held[index]
        sum_ref[...] = total
    for copy in across + late:
        copy.wait_recv()
    for copy in list(along_z.values()) + along_y + across + late:
        copy.wait_send()
    own.wait()


def gather_rows(piece, collective_id, packet=None):
    count = lax.axis_size("row")
    stat_rows, width = piece.shape
    copies = 4 * (count // 4) - 1
    summed = packet is not None
    vmem = pl.BlockSpec(memory_space=pltpu.VMEM)
    gathered = jax.ShapeDtypeStruct((count,) + piece.shape, piece.dtype)
    scratch = [
        pltpu.SemaphoreType.DMA,
        pltpu.SemaphoreType.DMA((copies,)),
        pltpu.SemaphoreType.DMA((copies,)),
    ]
    out_shape, out_specs = [gathered], [pl.BlockSpec(memory_space=pl.ANY)]
    if summed:
        out_shape.append(jax.ShapeDtypeStruct(packet.shape, packet.dtype))
        out_specs.append(vmem)
        scratch = [pltpu.VMEM((count,) + packet.shape, packet.dtype)] + scratch
        scratch += [pltpu.SemaphoreType.DMA((count - 1,)), pltpu.SemaphoreType.DMA((count - 1,))]
    operands = [piece] + ([packet] if summed else [])
    results = pl.pallas_call(
        functools.partial(gather_kernel, count, summed),
        out_shape=out_shape,
        in_specs=[vmem] * len(operands),
        out_specs=out_specs,
        scratch_shapes=scratch,
        compiler_params=pltpu.CompilerParams(collective_id=collective_id, has_side_effects=True),
    )(*operands)
    return [results[0].reshape(count * stat_rows, width)] + list(results[1:])


def shards(acts, grads, row_roots, col_stats):
    contract_first = (((0,), (0,)), ((), ()))
    block_size = row_roots.shape[1]
    weight_rows = grads.shape[1]
    weight_cols = acts.shape[1]
    stat_rows = col_stats.shape[0]
    block_count = weight_cols // block_size
    row_count = lax.axis_size("row")
    bits = row_count.bit_length() - 1
    total_rows = weight_rows * row_count
    me = lax.axis_index("row")
    other_grads = partner(grads, "row", 0)
    own_tile = lax.dot_general(
        grads, acts, contract_first, preferred_element_type=jnp.float32
    ).astype(jnp.bfloat16)
    other_tile = lax.dot_general(
        other_grads, acts, contract_first, preferred_element_type=jnp.float32
    ).astype(jnp.bfloat16)
    is_lower = me % 2 == 0
    paired = jnp.where(
        is_lower,
        jnp.concatenate([own_tile, other_tile], 0),
        jnp.concatenate([other_tile, own_tile], 0),
    )
    whitened = jnp.dot(row_roots, paired, preferred_element_type=jnp.float32).astype(jnp.bfloat16)
    mix = (1.0 - decay_rate) / total_rows
    first_row = me * stat_rows
    row_iota = lax.broadcasted_iota(jnp.int32, (stat_rows, block_size), 0) + first_row
    col_iota = lax.broadcasted_iota(jnp.int32, (stat_rows, block_size), 1)
    on_diagonal = row_iota == col_iota
    identity_rows = on_diagonal.astype(jnp.float32)

    def block(array, index):
        return array[:, index * block_size : (index + 1) * block_size]

    blocks = range(block_count)
    old_diagonal = jnp.concatenate(
        [jnp.sum(jnp.where(on_diagonal, block(col_stats, k), 0.0), 0) for k in blocks]
    )
    squares = jnp.sum(jnp.square(whitened.astype(jnp.float32)), 0)
    packet = (decay_rate * old_diagonal + mix * squares).reshape(-1, 128)

    stats = []
    for k in blocks:
        columns = block(whitened, k)
        part = lax.dot_general(columns, columns, contract_first, preferred_element_type=jnp.float32)
        summed = reduce_rows(part.astype(jnp.bfloat16), k, me, bits, stat_rows)
        mixed = decay_rate * block(col_stats, k) + mix * summed
        stats.append(jnp.where(on_diagonal, 0.0, mixed))
    off_full, diagonal = gather_rows(jnp.concatenate(stats, 1).astype(jnp.bfloat16), 0, packet)
    diagonal = diagonal.reshape(block_count, block_size)
    stats = [jnp.where(on_diagonal, diagonal[k][None], stats[k]) for k in blocks]
    new_stats = jnp.concatenate(stats, 1)

    root_pieces = []
    for k in blocks:
        off = block(off_full, k)
        shifted = diagonal[k] + damping
        scale = 2.0 * jnp.sum(shifted) / block_size

        def times_start(rows):
            high = rows.astype(jnp.bfloat16)
            low = (rows - high.astype(jnp.float32)).astype(jnp.bfloat16)
            both = jnp.dot(
                jnp.concatenate([high, low], 0), off, preferred_element_type=jnp.float32
            )
            return (both[:stat_rows] + both[stat_rows:] + rows * shifted[None]) / scale

        start_rows = jnp.where(on_diagonal, shifted[None], stats[k]) / scale
        first = 1.5 * identity_rows - 0.5 * start_rows
        step = times_start(first)
        product_rows = 1.5 * step - 0.5 * times_start(step)
        second = 1.5 * identity_rows - 0.5 * product_rows
        root_rows = 1.5 * second - 0.5 * times_start(second)
        root_pieces.append(root_rows / jnp.sqrt(scale))
    new_roots = jnp.concatenate(root_pieces, 1)
    (roots_full,) = gather_rows(new_roots.astype(jnp.bfloat16), 2)
    terms = []
    for k in blocks:
        right = block(roots_full, k)
        terms.append(jnp.dot(block(whitened, k), right, preferred_element_type=jnp.float32))
    product = jnp.concatenate(terms, 1)
    grad_square = jnp.sum(jnp.square(own_tile.astype(jnp.float32)))
    prod_square = sum(jnp.sum(jnp.square(term)) for term in terms)
    lane = lax.broadcasted_iota(jnp.int32, (8, 128), 1)
    norms = jnp.where(lane == 0, grad_square, jnp.where(lane == 1, prod_square, 0.0))
    totals = small_sum(norms, ("row", "col"), 1)
    update = (product * jnp.sqrt(totals[0, 0] / (totals[0, 1] + epsilon))).astype(jnp.bfloat16)
    return (update, new_stats, new_roots)


def solution(mesh):
    return jax.shard_map(
        shards,
        mesh=mesh,
        in_specs=(P(None, "col"), P(None, "row"), P("row", None), P("row", "col")),
        out_specs=(P("row", "col"), P("row", "col"), P("row", "col")),
        check_vma=False,
    )
```

```python
import functools

import jax
import jax.numpy as jnp
from jax import lax
from jax.experimental import pallas as pl
from jax.experimental.pallas import tpu as pltpu
from jax.sharding import PartitionSpec as P


decay_rate = 0.75
damping = 0.001
epsilon = 1e-06


def partner(block, axis, bit):
    count = lax.axis_size(axis)
    route = []
    for low in range(count):
        high = low | 1 << bit
        if high != low and high < count:
            route += [(low, high), (high, low)]
    return lax.ppermute(block, axis, route)


def exchange_kernel(axes, sizes, x_ref, out_ref, held, send_sems, recv_sems):
    count = 1
    me = 0
    for axis, size in zip(axes, sizes):
        me = me * size + lax.axis_index(axis)
        count *= size

    def place(peer):
        spot = {}
        for axis, size in reversed(list(zip(axes, sizes))):
            spot[axis] = lax.rem(peer, size)
            peer = lax.div(peer, size)
        return spot

    peers = [place(lax.rem(me + step, count)) for step in range(1, count)]
    barrier = pltpu.get_barrier_semaphore()
    for peer in peers:
        pl.semaphore_signal(barrier, inc=1, device_id=peer, device_id_type=pl.DeviceIdType.MESH)
    pl.semaphore_wait(barrier, count - 1)
    copies = []
    for index, peer in enumerate(peers):
        copy = pltpu.make_async_remote_copy(
            src_ref=x_ref,
            dst_ref=held.at[me],
            send_sem=send_sems.at[index],
            recv_sem=recv_sems.at[index],
            device_id=peer,
            device_id_type=pl.DeviceIdType.MESH,
        )
        copy.start()
        copies.append(copy)
    held[me] = x_ref[...]
    for copy in copies:
        copy.wait()
    total = held[0]
    for index in range(1, count):
        total = total + held[index]
    out_ref[...] = total


def small_sum(packet, axes, collective_id):
    sizes = tuple(lax.axis_size(axis) for axis in axes)
    count = 1
    for size in sizes:
        count *= size
    return pl.pallas_call(
        functools.partial(exchange_kernel, axes, sizes),
        out_shape=jax.ShapeDtypeStruct(packet.shape, packet.dtype),
        in_specs=[pl.BlockSpec(memory_space=pltpu.VMEM)],
        out_specs=pl.BlockSpec(memory_space=pltpu.VMEM),
        scratch_shapes=[
            pltpu.VMEM((count,) + packet.shape, packet.dtype),
            pltpu.SemaphoreType.DMA((count - 1,)),
            pltpu.SemaphoreType.DMA((count - 1,)),
        ],
        compiler_params=pltpu.CompilerParams(collective_id=collective_id, has_side_effects=True),
    )(packet)


def bit_orders(index_block, bits):
    far = list(range(2, bits))
    if index_block % 2 == 0:
        return [0, 1] + far
    return [0] + far + [1]


def halve(parts, mine, bit, position):
    low = lax.index_in_dim(parts, 0, position, keepdims=False)
    high = lax.index_in_dim(parts, 1, position, keepdims=False)
    upper = mine == 1
    keep = jnp.where(upper, high, low)
    send = jnp.where(upper, low, high).astype(jnp.bfloat16)
    return keep.astype(jnp.float32) + partner(send, "row", bit).astype(jnp.float32)


def reduce_rows(part, index_block, me, bits, stat_rows):
    width = part.shape[1]
    left = list(range(bits - 1, -1, -1))
    current = part.reshape((2,) * bits + (stat_rows, width))
    for bit in bit_orders(index_block, bits):
        position = left.index(bit)
        left.remove(bit)
        current = halve(current, (me >> bit) & 1, bit, position)
    return current


def gather_kernel(count, summed, x_ref, *refs):
    if summed:
        packet_ref, out_ref, sum_ref, held, own_sem, sends, recvs, small_sends, small_recvs = refs
    else:
        out_ref, own_sem, sends, recvs = refs
    depth = count // 4
    me = lax.axis_index("row")
    mesh_ids = pl.DeviceIdType.MESH
    near = lax.rem(me, 4)
    tall = lax.div(me, 4)
    y_peer = me + 2 - 4 * lax.rem(lax.div(me, 2), 2)
    core_peer = me + 1 - 2 * lax.rem(me, 2)
    origins = [lax.bitwise_xor(tall, step) * 4 + near for step in range(depth)]
    y_origins = [lax.bitwise_xor(tall, step) * 4 + lax.rem(near + 2, 4) for step in range(depth)]
    hops = [1 << bit for bit in range(depth.bit_length() - 1)]
    z_peers = [origins[hop] for hop in hops]
    everyone = [lax.rem(me + step, count) for step in range(1, count)]
    greeted = everyone if summed else z_peers + [y_peer, core_peer]
    barrier = pltpu.get_barrier_semaphore()
    for peer in greeted:
        pl.semaphore_signal(barrier, inc=1, device_id={"row": peer}, device_id_type=mesh_ids)
    pl.semaphore_wait(barrier, len(greeted))

    def push(source, slot, peer, index):
        copy = pltpu.make_async_remote_copy(
            src_ref=source,
            dst_ref=out_ref.at[slot],
            send_sem=sends.at[index],
            recv_sem=recvs.at[index],
            device_id={"row": peer},
            device_id_type=mesh_ids,
        )
        copy.start()
        return copy

    small = []
    if summed:
        for index, peer in enumerate(everyone):
            copy = pltpu.make_async_remote_copy(
                src_ref=packet_ref,
                dst_ref=held.at[me],
                send_sem=small_sends.at[index],
                recv_sem=small_recvs.at[index],
                device_id={"row": peer},
                device_id_type=mesh_ids,
            )
            copy.start()
            small.append(copy)
        held[me] = packet_ref[...]
    along_z = {hop: push(x_ref, me, origins[hop], hop - 1) for hop in hops}
    base = depth - 1
    along_y = [push(x_ref, me, y_peer, base)]
    across = [push(x_ref, me, core_peer, base + depth)]
    own = pltpu.make_async_copy(x_ref, out_ref.at[me], own_sem)
    own.start()
    late = []

    def forward_y(step):
        along_y[step].wait_recv()
        slot = y_origins[step]
        late.append(push(out_ref.at[slot], slot, core_peer, base + 2 * depth + step))

    for step in range(1, depth):
        along_z[step].wait_recv()
        slot = origins[step]
        for hop in hops:
            if hop < (step & -step):
                along_z[step + hop] = push(out_ref.at[slot], slot, origins[hop], step + hop - 1)
        along_y.append(push(out_ref.at[slot], slot, y_peer, base + step))
        across.append(push(out_ref.at[slot], slot, core_peer, base + depth + step))
        forward_y(step - 1)
    forward_y(depth - 1)
    if summed:
        for copy in small:
            copy.wait()
        total = held[0]
        for index in range(1, count):
            total = total + held[index]
        sum_ref[...] = total
    for copy in across + late:
        copy.wait_recv()
    for copy in list(along_z.values()) + along_y + across + late:
        copy.wait_send()
    own.wait()


def gather_rows(piece, collective_id, packet=None):
    count = lax.axis_size("row")
    stat_rows, width = piece.shape
    copies = 4 * (count // 4) - 1
    summed = packet is not None
    vmem = pl.BlockSpec(memory_space=pltpu.VMEM)
    gathered = jax.ShapeDtypeStruct((count,) + piece.shape, piece.dtype)
    scratch = [
        pltpu.SemaphoreType.DMA,
        pltpu.SemaphoreType.DMA((copies,)),
        pltpu.SemaphoreType.DMA((copies,)),
    ]
    out_shape, out_specs = [gathered], [pl.BlockSpec(memory_space=pl.ANY)]
    if summed:
        out_shape.append(jax.ShapeDtypeStruct(packet.shape, packet.dtype))
        out_specs.append(vmem)
        scratch = [pltpu.VMEM((count,) + packet.shape, packet.dtype)] + scratch
        scratch += [pltpu.SemaphoreType.DMA((count - 1,)), pltpu.SemaphoreType.DMA((count - 1,))]
    operands = [piece] + ([packet] if summed else [])
    results = pl.pallas_call(
        functools.partial(gather_kernel, count, summed),
        out_shape=out_shape,
        in_specs=[vmem] * len(operands),
        out_specs=out_specs,
        scratch_shapes=scratch,
        compiler_params=pltpu.CompilerParams(collective_id=collective_id, has_side_effects=True),
    )(*operands)
    return [results[0].reshape(count * stat_rows, width)] + list(results[1:])


TILE = 128


def tile_of(shape, dimension, first=0):
    return lax.div(lax.broadcasted_iota(jnp.int32, shape, dimension) + first, TILE)


def pack_pair(upper, lower, first_row):
    width = upper.shape[1] + TILE
    shape = (upper.shape[0], width)
    return jnp.where(
        tile_of(shape, 1) <= tile_of(shape, 0, first_row),
        jnp.pad(lower, ((0, 0), (0, TILE))),
        jnp.pad(upper, ((0, 0), (TILE, 0))),
    )


def unpack_pair(packed):
    size = packed.shape[0]
    shape = (size, size)
    upper, lower = packed[:, TILE:], packed[:, :size]
    row_tile, col_tile = tile_of(shape, 0), tile_of(shape, 1)
    return [
        jnp.where(col_tile >= row_tile, upper, upper.T),
        jnp.where(col_tile <= row_tile, lower, lower.T),
    ]


def gather_symmetric(pieces, first_row, collective_id, packet=None):
    pieces = [piece.astype(jnp.bfloat16) for piece in pieces]
    size = pieces[0].shape[1]
    paired = len(pieces) // 2 * 2
    packed = [
        pack_pair(pieces[k], pieces[k + 1], first_row) for k in range(0, paired, 2)
    ] + pieces[paired:]
    results = gather_rows(jnp.concatenate(packed, 1), collective_id, packet)
    full = []
    for k in range(0, paired, 2):
        start = k // 2 * (size + TILE)
        full += unpack_pair(results[0][:, start : start + size + TILE])
    if paired < len(pieces):
        full.append(results[0][:, -size:])
    return [full] + results[1:]


def shards(acts, grads, row_roots, col_stats):
    contract_first = (((0,), (0,)), ((), ()))
    block_size = row_roots.shape[1]
    weight_rows = grads.shape[1]
    weight_cols = acts.shape[1]
    stat_rows = col_stats.shape[0]
    block_count = weight_cols // block_size
    row_count = lax.axis_size("row")
    bits = row_count.bit_length() - 1
    total_rows = weight_rows * row_count
    me = lax.axis_index("row")
    other_grads = partner(grads, "row", 0)
    own_tile = lax.dot_general(
        grads, acts, contract_first, preferred_element_type=jnp.float32
    ).astype(jnp.bfloat16)
    other_tile = lax.dot_general(
        other_grads, acts, contract_first, preferred_element_type=jnp.float32
    ).astype(jnp.bfloat16)
    is_lower = me % 2 == 0
    paired = jnp.where(
        is_lower,
        jnp.concatenate([own_tile, other_tile], 0),
        jnp.concatenate([other_tile, own_tile], 0),
    )
    whitened = jnp.dot(row_roots, paired, preferred_element_type=jnp.float32).astype(jnp.bfloat16)
    mix = (1.0 - decay_rate) / total_rows
    first_row = me * stat_rows
    row_iota = lax.broadcasted_iota(jnp.int32, (stat_rows, block_size), 0) + first_row
    col_iota = lax.broadcasted_iota(jnp.int32, (stat_rows, block_size), 1)
    on_diagonal = row_iota == col_iota
    identity_rows = on_diagonal.astype(jnp.float32)

    def block(array, index):
        return array[:, index * block_size : (index + 1) * block_size]

    blocks = range(block_count)
    old_diagonal = jnp.concatenate(
        [jnp.sum(jnp.where(on_diagonal, block(col_stats, k), 0.0), 0) for k in blocks]
    )
    squares = jnp.sum(jnp.square(whitened.astype(jnp.float32)), 0)
    packet = (decay_rate * old_diagonal + mix * squares).reshape(-1, 128)

    stats = []
    for k in blocks:
        columns = block(whitened, k)
        part = lax.dot_general(columns, columns, contract_first, preferred_element_type=jnp.float32)
        summed = reduce_rows(part.astype(jnp.bfloat16), k, me, bits, stat_rows)
        mixed = decay_rate * block(col_stats, k) + mix * summed
        stats.append(jnp.where(on_diagonal, 0.0, mixed))
    off_full, diagonal = gather_symmetric(stats, first_row, 0, packet)
    diagonal = diagonal.reshape(block_count, block_size)
    stats = [jnp.where(on_diagonal, diagonal[k][None], stats[k]) for k in blocks]
    new_stats = jnp.concatenate(stats, 1)

    root_pieces = []
    for k in blocks:
        off = off_full[k]
        shifted = diagonal[k] + damping
        scale = 2.0 * jnp.sum(shifted) / block_size

        def times_start(rows):
            high = rows.astype(jnp.bfloat16)
            low = (rows - high.astype(jnp.float32)).astype(jnp.bfloat16)
            both = jnp.dot(
                jnp.concatenate([high, low], 0), off, preferred_element_type=jnp.float32
            )
            return (both[:stat_rows] + both[stat_rows:] + rows * shifted[None]) / scale

        start_rows = jnp.where(on_diagonal, shifted[None], stats[k]) / scale
        first = 1.5 * identity_rows - 0.5 * start_rows
        step = times_start(first)
        product_rows = 1.5 * step - 0.5 * times_start(step)
        second = 1.5 * identity_rows - 0.5 * product_rows
        root_rows = 1.5 * second - 0.5 * times_start(second)
        root_pieces.append(root_rows / jnp.sqrt(scale))
    new_roots = jnp.concatenate(root_pieces, 1)
    (roots_full,) = gather_symmetric(root_pieces, first_row, 2)
    terms = []
    for k in blocks:
        right = roots_full[k]
        terms.append(jnp.dot(block(whitened, k), right, preferred_element_type=jnp.float32))
    product = jnp.concatenate(terms, 1)
    grad_square = jnp.sum(jnp.square(own_tile.astype(jnp.float32)))
    prod_square = sum(jnp.sum(jnp.square(term)) for term in terms)
    lane = lax.broadcasted_iota(jnp.int32, (8, 128), 1)
    norms = jnp.where(lane == 0, grad_square, jnp.where(lane == 1, prod_square, 0.0))
    totals = small_sum(norms, ("row", "col"), 1)
    update = (product * jnp.sqrt(totals[0, 0] / (totals[0, 1] + epsilon))).astype(jnp.bfloat16)
    return (update, new_stats, new_roots)


def solution(mesh):
    return jax.shard_map(
        shards,
        mesh=mesh,
        in_specs=(P(None, "col"), P(None, "row"), P("row", None), P("row", "col")),
        out_specs=(P("row", "col"), P("row", "col"), P("row", "col")),
        check_vma=False,
    )
```
